32 devices in a mesh: row: 4 (over z), col: 8 (over y, x, core).
Axes of the slice: x: 2, y: 2, z: 4, core: 2. Of those that a mesh axis runs over, the one named last changes fastest.
Arguments:
- a_blocks: bfloat16 [4, 8, 108, 138, 138], P('row', 'col'), may hold values from -0.0625 to 0.0625
- a_coord: int32 [4, 8, 108], replicated, may hold values from 0 to 1151, as said below
- b_blocks: bfloat16 [4, 2, 8, 27, 138, 138], P('row', None, 'col'), may hold values from -6 to 6
- b_coord: int32 [4, 2, 8, 27], replicated, may hold values from 0 to 287, as said below
- keep_list: int32 [4, 8, 32], replicated, may hold values from 0 to 63, as said below
- permutation: int32 [64], replicated, may hold values from 0 to 63, as said below
Outputs:
- next_rows: bfloat16 [4, 8, 16, 4, 138, 138], P('row', 'col')
The draws below stay inside these ranges and needn't reach their ends.
Inputs may be any that keep to these rules, and one draw needn't show every extreme that they name: `a_coord`: codes block (i, k) as i * 72 + k; the entries of one device are distinct; over all devices and both A and B the block columns k take only 18 values, among them 0 and 71. `b_coord`: codes block (k, j) as k * 4 + j; the entries of one device and panel are distinct; k takes the same 18 values as in a_coord. `keep_list`: codes product block (i, j) as i * 4 + j; the entries of one device are distinct. A permutation; the 16 block rows of one device row go to 4 device rows, exactly 4 to each.
All inputs are finite; a program needn't handle non-finite values.
Results may differ from the reference program's by a relative error of at most 0.001.
Values may be sent and summed in bfloat16 or wider, within the bound.
A program may use at most 256 MiB of HBM per device.

```python
import jax
import jax.numpy as jnp
from jax import lax

BS = 138
KL = 72
BRL = 16
BCL = 4
GRID_R = 4
GRID_C = 8
CAP = 4
HOT = 18
SA = 108
SB = 27
KEEP = 32
NBR = 64


def distinct_codes(key, grid_count, total):
    first_key, second_key = jax.random.split(key)
    inner = jax.random.permutation(first_key, total - 2)[:grid_count - 2].astype(jnp.int32) + 1
    ends = jnp.array([0, total - 1], jnp.int32)
    return jax.random.permutation(second_key, jnp.concatenate([ends, inner]))


def code_table(key, salt, tables, grid_count, total):
    keys = jax.random.split(jax.random.fold_in(key, salt), tables)
    return jax.vmap(lambda single: distinct_codes(single, grid_count, total))(keys)


def hot_columns(key):
    inner = jax.random.permutation(jax.random.fold_in(key, 5), KL - 2)[:HOT - 2].astype(jnp.int32) + 1
    return jnp.concatenate([jnp.array([0], jnp.int32), inner, jnp.array([KL - 1], jnp.int32)])


def draw_a_coord(key, part):
    columns = hot_columns(key)
    picks = code_table(key, 11, GRID_R * GRID_C, SA, BRL * HOT)
    codes = picks // HOT * KL + columns[picks % HOT]
    return codes.reshape(GRID_R, GRID_C, SA).astype(jnp.int32)


def draw_b_coord(key, part):
    columns = hot_columns(key)
    picks = code_table(key, 13, GRID_R * 2 * GRID_C, SB, HOT * BCL)
    codes = columns[picks // BCL] * BCL + picks % BCL
    return codes.reshape(GRID_R, 2, GRID_C, SB).astype(jnp.int32)


def draw_keep_list(key, part):
    return code_table(key, 17, GRID_R * GRID_C, KEEP, BRL * BCL).reshape(GRID_R, GRID_C, KEEP)


def draw_permutation(key, part):
    base = jax.random.fold_in(key, 23)
    rho_key, offset_key, local_key, place_key = jax.random.split(base, 4)
    rho = jax.random.permutation(rho_key, GRID_R).astype(jnp.int32)
    offsets = jax.random.permutation(offset_key, GRID_R)[:BRL // CAP].astype(jnp.int32)
    local_order = jax.vmap(lambda single: jax.random.permutation(single, BRL))(jax.random.split(local_key, GRID_R)).astype(jnp.int32)
    new_places = jax.vmap(lambda single: jax.random.permutation(single, BRL))(jax.random.split(place_key, GRID_R)).astype(jnp.int32)
    source_rows = jnp.arange(GRID_R, dtype=jnp.int32)[:, None]
    group_index = local_order // CAP
    within = local_order % CAP
    owners = (rho[source_rows] + offsets[group_index]) % GRID_R
    places = new_places[owners, CAP * group_index + within]
    return (owners * BRL + places).reshape(-1).astype(jnp.int32)


def level_of(key, dims, cuts, low, high):
    factor_of, own = 1.0, jax.random.fold_in(key, 6)
    for axis_at, blocks in cuts:
        heights = jnp.exp(jax.random.uniform(jax.random.fold_in(own, axis_at), (blocks,), jnp.float32, low / len(cuts), high / len(cuts)))
        factor_of = factor_of * jnp.repeat(heights, dims[axis_at] // blocks).reshape([-1 if axis == axis_at else 1 for axis in range(len(dims))])
    return factor_of


def gaussian(key, dims, spread, bound, shards=(), held_as=jnp.bfloat16):
    loudness = level_of(key, dims, shards, -0.22, 0.18) if shards else 1.0
    drawn = jax.random.normal(key, dims, jnp.float32) * spread * loudness
    return jnp.minimum(jnp.maximum(drawn, -bound), bound).astype(held_as)


def setup_inputs(seed: int = 0) -> dict:
    seeds = jax.random.split(jax.random.key(seed), 7)
    return {
        "a_blocks": gaussian(seeds[0], (GRID_R, GRID_C, SA, BS, BS), (KL * BS) ** -0.5, 0.0625, ((0, 4), (1, 8))),
        "a_coord": draw_a_coord(jax.random.fold_in(seeds[6], 71), 0),
        "b_blocks": gaussian(seeds[2], (GRID_R, 2, GRID_C, SB, BS, BS), 1.0, 6.0, ((0, 4), (2, 8))),
        "b_coord": draw_b_coord(jax.random.fold_in(seeds[6], 71), 0),
        "keep_list": draw_keep_list(jax.random.fold_in(seeds[6], 71), 0),
        "permutation": draw_permutation(jax.random.fold_in(seeds[6], 71), 0),
    }


def fill_grid(blocks, block_codes, grid_count):
    blank_grid = jnp.zeros((grid_count,) + blocks.shape[1:], blocks.dtype)
    return blank_grid.at[block_codes].set(blocks)


def stop_term(a_part, a_codes, b_part, b_codes):
    a_grid = fill_grid(a_part, a_codes, BRL * KL).reshape(BRL, KL, BS, BS).astype(jnp.float32)
    b_grid = fill_grid(b_part, b_codes, KL * BCL).reshape(KL, BCL, BS, BS).astype(jnp.float32)
    return jnp.einsum("ikab,kjbc->ijac", a_grid, b_grid, precision=lax.Precision.HIGHEST)


def reference(a_blocks, a_coord, b_blocks, b_coord, keep_list, permutation):
    device_count = GRID_R * GRID_C
    a_later = jnp.roll(a_blocks, -1, axis=1)
    a_later_codes = jnp.roll(a_coord, -1, axis=1)
    b_first = b_blocks[:, 0]
    b_first_codes = b_coord[:, 0]
    b_later = jnp.concatenate([b_blocks[1:, 0], b_blocks[:1, 1]], axis=0)
    b_later_codes = jnp.concatenate([b_coord[1:, 0], b_coord[:1, 1]], axis=0)

    def flatten(array):
        return array.reshape((device_count,) + array.shape[2:])

    def one_device(items):
        a_now, a_now_codes, a_next, a_next_codes, b_now, b_now_codes, b_next, b_next_codes, kept = items
        product = stop_term(a_now, a_now_codes, b_now, b_now_codes) + stop_term(a_next, a_next_codes, b_next, b_next_codes)
        all_codes = jnp.arange(BRL * BCL, dtype=jnp.int32)
        keep_mask = jnp.any(all_codes[:, None] == kept[None, :], axis=1).reshape(BRL, BCL)
        return jnp.where(keep_mask[:, :, None, None], product, jnp.float32(0.0)).astype(jnp.bfloat16)

    filtered = lax.map(one_device, (flatten(a_blocks), flatten(a_coord), flatten(a_later), flatten(a_later_codes),
                                    flatten(b_first), flatten(b_first_codes), flatten(b_later), flatten(b_later_codes),
                                    flatten(keep_list)))
    filtered = filtered.reshape(GRID_R, GRID_C, BRL, BCL, BS, BS).transpose(0, 2, 1, 3, 4, 5)
    block_rows = filtered.reshape(NBR, GRID_C, BCL, BS, BS)
    moved = jnp.zeros_like(block_rows).at[permutation].set(block_rows)
    return moved.reshape(GRID_R, BRL, GRID_C, BCL, BS, BS).transpose(0, 2, 1, 3, 4, 5)
```

```python
import jax
import jax.numpy as jnp
from jax import lax
from jax.experimental import pallas as pl
from jax.experimental.pallas import tpu as pltpu
from jax.sharding import PartitionSpec as P

KL = 72
BRL = 16
BCL = 4
LANES = 128
SMEM = pl.BlockSpec(memory_space=pltpu.SMEM)
VMEM = pl.BlockSpec(memory_space=pltpu.VMEM)


def shifted(value, axis, steps):
    count = lax.axis_size(axis)
    pairs = [(source, (source + steps) % count) for source in range(count)]
    return lax.ppermute(value, axis, pairs)


def strip_kernel(home_ref, col_ref, main_ref, rest_ref, out_ref):
    out_ref[...] = jnp.zeros_like(out_ref)
    rest = rest_ref.shape[-1]

    def step(t, carry):
        home, j = home_ref[t], col_ref[t]
        out_ref[home, :, pl.ds(pl.multiple_of(j * LANES, LANES), LANES)] = main_ref[t]
        tail = rest_ref[t]
        for at in range(BCL):

            @pl.when(j == at)
            def _():
                out_ref[home, :, BCL * LANES + at * rest : BCL * LANES + (at + 1) * rest] = tail

        return carry

    lax.fori_loop(0, main_ref.shape[0], step, 0)


def build_strips(main, rest, home, col):
    slots, edge, _ = main.shape
    return pl.pallas_call(
        strip_kernel,
        out_shape=jax.ShapeDtypeStruct((slots + 1, edge, (BCL + 1) * LANES), jnp.bfloat16),
        in_specs=[SMEM, SMEM, VMEM, VMEM],
        out_specs=VMEM,
        name="strips",
    )(home, col, main, rest)


def first_kernel(row_ref, home_ref, a_ref, strip_ref, acc_ref):
    acc_ref[...] = jnp.zeros_like(acc_ref)

    def step(s, carry):
        i = row_ref[s]
        acc_ref[i] += jnp.dot(a_ref[s], strip_ref[home_ref[s]], preferred_element_type=jnp.float32)
        return carry

    lax.fori_loop(0, a_ref.shape[0], step, 0)


def second_kernel(row_ref, home_ref, place_ref, a_ref, strip_ref, start_ref, mask_ref, out_ref, acc_ref):
    acc_ref[...] = start_ref[...]

    def step(s, carry):
        i = row_ref[s]
        acc_ref[i] += jnp.dot(a_ref[s], strip_ref[home_ref[s]], preferred_element_type=jnp.float32)
        return carry

    lax.fori_loop(0, a_ref.shape[0], step, 0)

    def put(i, carry):
        kept = jnp.where(mask_ref[i] > 0.0, acc_ref[i], 0.0)
        out_ref[place_ref[i]] = kept.astype(jnp.bfloat16)
        return carry

    lax.fori_loop(0, acc_ref.shape[0], put, 0)


def cost(a, width):
    slots, rows, depth = a.shape
    return pl.CostEstimate(
        flops=2 * slots * rows * 256 * 768, bytes_accessed=8_000_000, transcendentals=0
    )


def first_stop(a, rows, homes, strips):
    width = strips.shape[-1]
    return pl.pallas_call(
        first_kernel,
        out_shape=jax.ShapeDtypeStruct((BRL, a.shape[1], width), jnp.float32),
        in_specs=[SMEM, SMEM, VMEM, VMEM],
        out_specs=VMEM,
        cost_estimate=cost(a, width),
        name="first_stop",
    )(rows, homes, a, strips)


def second_stop(a, rows, homes, place, strips, start, mask):
    width = strips.shape[-1]
    return pl.pallas_call(
        second_kernel,
        out_shape=jax.ShapeDtypeStruct((BRL, a.shape[1], width), jnp.bfloat16),
        in_specs=[SMEM, SMEM, SMEM, VMEM, VMEM, VMEM, VMEM],
        out_specs=VMEM,
        scratch_shapes=[pltpu.VMEM((BRL, a.shape[1], width), jnp.float32)],
        cost_estimate=cost(a, width),
        name="second_stop",
    )(rows, homes, place, a, strips, start, mask)


def unpack_kernel(src_ref, in_ref, out_ref):
    rest = out_ref.shape[-1] - LANES

    def step(l, carry):
        strip = in_ref[src_ref[l]]
        for j in range(BCL):
            out_ref[l, j, :, 0:LANES] = strip[:, j * LANES : (j + 1) * LANES]
            out_ref[l, j, :, LANES:] = strip[:, BCL * LANES + j * rest : BCL * LANES + (j + 1) * rest]
        return carry

    lax.fori_loop(0, out_ref.shape[0], step, 0)


def unpack(arrived, source, edge):
    return pl.pallas_call(
        unpack_kernel,
        out_shape=jax.ShapeDtypeStruct((BRL, BCL, arrived.shape[1], edge), jnp.bfloat16),
        in_specs=[SMEM, VMEM],
        out_specs=VMEM,
        name="unpack",
    )(source, arrived)


def homes_of(a_codes, b_codes):
    b_rows = b_codes // BCL
    slots = jnp.arange(b_codes.shape[0], dtype=jnp.int32)
    none = jnp.int32(b_codes.shape[0])

    def first_match(wanted):
        return jnp.min(jnp.where(wanted[:, None] == b_rows[None, :], slots[None, :], none), axis=1)

    return a_codes // KL, first_match(a_codes % KL), first_match(b_rows), b_codes % BCL


def body(a_blocks, a_coord, b_blocks, b_coord, keep_list, permutation):
    row_count = lax.axis_size("row")
    col_count = lax.axis_size("col")
    slot_count = BRL // row_count
    row_here = lax.axis_index("row")
    col_here = lax.axis_index("col")
    row_next = (row_here + 1) % row_count
    col_next = (col_here + 1) % col_count
    edge = a_blocks.shape[-1]
    parts = 3 if edge % 3 == 0 else 1
    size = edge // parts

    a_turned = a_blocks[0, 0].transpose(1, 2, 0)
    a_parts = [a_turned[q * size : (q + 1) * size] for q in range(parts)]

    b_first = b_blocks[0, 0, 0]
    b_sent = jnp.where(row_here == 0, b_blocks[0, 1, 0], b_first)
    sent_rest = b_sent[:, :, LANES:].transpose(1, 0, 2).reshape(edge, -1)
    moved_main = shifted(b_sent[:, :, :LANES], "row", -1)
    moved_rest = shifted(sent_rest, "row", -1)
    moved_rest = moved_rest.reshape(edge, b_first.shape[0], -1).transpose(1, 0, 2)
    a_moved = [shifted(part, "col", -1) for part in a_parts]

    rows1, homes1, b_homes1, b_cols1 = homes_of(
        a_coord[row_here, col_here], b_coord[row_here, 0, col_here]
    )
    image_pick = (row_next == 0).astype(jnp.int32)
    rows2, homes2, b_homes2, b_cols2 = homes_of(
        a_coord[row_here, col_next], b_coord[row_next, image_pick, col_here]
    )
    own_keep = keep_list[row_here, col_here]
    all_codes = jnp.arange(BRL * BCL, dtype=jnp.int32)
    keep_mask = jnp.any(all_codes[:, None] == own_keep[None, :], axis=1).reshape(BRL, BCL)
    keep_mask = keep_mask.astype(jnp.float32)
    rest = edge - LANES
    mask = jnp.concatenate(
        [
            jnp.repeat(keep_mask, LANES, axis=1),
            jnp.repeat(keep_mask, rest, axis=1),
            jnp.zeros((BRL, LANES - BCL * rest), jnp.float32),
        ],
        axis=1,
    )[:, None, :]

    targets = permutation.reshape(row_count, BRL)
    owners = targets // BRL
    positions = jnp.arange(BRL, dtype=jnp.int32)
    before = (owners[:, None, :] == owners[:, :, None]) & (
        positions[None, None, :] < positions[None, :, None]
    )
    slot_rank = jnp.sum(before.astype(jnp.int32), axis=2)
    place = owners[row_here] * slot_count + slot_rank[row_here]
    all_rows = jnp.arange(permutation.shape[0], dtype=jnp.int32)
    wanted = row_here * BRL + positions
    arrival = all_rows // BRL * slot_count + slot_rank.reshape(-1)
    source = jnp.sum(
        jnp.where(permutation[None, :] == wanted[:, None], arrival[None, :], 0), axis=1
    )

    strips1 = build_strips(b_first[:, :, :LANES], b_first[:, :, LANES:], b_homes1, b_cols1)
    starts = [first_stop(part.transpose(2, 0, 1), rows1, homes1, strips1) for part in a_parts]
    strips2 = build_strips(moved_main, moved_rest, b_homes2, b_cols2)
    done = []
    for q in range(parts):
        out = second_stop(
            a_moved[q].transpose(2, 0, 1), rows2, homes2, place, strips2, starts[q], mask
        )
        out = out.reshape((row_count, slot_count) + out.shape[1:])
        incoming = lax.all_to_all(out, "row", split_axis=0, concat_axis=0, tiled=True)
        done.append(unpack(incoming.reshape((BRL,) + incoming.shape[2:]), source, edge))
    return jnp.concatenate(done, axis=2)[None, None]


def solution(mesh):
    in_specs = (
        P("row", "col", None, None, None),
        P(),
        P("row", None, "col", None, None, None),
        P(),
        P(),
        P(),
    )
    out_specs = P("row", "col", None, None, None, None)
    return jax.shard_map(body, mesh=mesh, in_specs=in_specs, out_specs=out_specs, check_vma=False)
```

```python
import jax
import jax.numpy as jnp
from jax import lax
from jax.experimental.layout import Layout, with_layout_constraint
from jax.experimental import pallas as pl
from jax.experimental.pallas import tpu as pltpu
from jax.sharding import PartitionSpec as P

KL = 72
BRL = 16
BCL = 4
LANES = 128
UNROLL = 4
SMEM = pl.BlockSpec(memory_space=pltpu.SMEM)
VMEM = pl.BlockSpec(memory_space=pltpu.VMEM)


def shifted(value, axis, steps):
    count = lax.axis_size(axis)
    pairs = [(source, (source + steps) % count) for source in range(count)]
    return lax.ppermute(value, axis, pairs)


def list_kernel(match_ref, item_ref, found_ref, count_ref):
    def step(n, at):
        slot = match_ref[n]
        item_ref[at] = n
        found_ref[at] = slot
        return at + (slot >= 0).astype(jnp.int32)

    total = lax.fori_loop(0, match_ref.shape[0], step, jnp.int32(0), unroll=8)
    count_ref[0] = total
    for extra in range(UNROLL):
        item_ref[total + extra] = -1
        found_ref[total + extra] = 0


def list_pairs(match):
    length = match.shape[0] + UNROLL
    shape = jax.ShapeDtypeStruct((length,), jnp.int32)
    return pl.pallas_call(
        list_kernel,
        out_shape=(shape, shape, jax.ShapeDtypeStruct((1,), jnp.int32)),
        in_specs=[SMEM],
        out_specs=(SMEM, SMEM, SMEM),
        name="list_pairs",
    )(match)


def add_pairs(item_ref, found_ref, count_ref, row_ref, a_ref, b_ref, acc_ref):
    spare = acc_ref.shape[0] - 1

    def step(block, carry):
        terms, places = [], []
        for u in range(UNROLL):
            item = item_ref[block * UNROLL + u]
            real = item >= 0
            safe = jnp.maximum(item, 0)
            s = safe // BCL
            places.append(jnp.where(real, row_ref[s] * BCL + safe % BCL, spare))
            terms.append(
                jnp.dot(
                    a_ref[s],
                    b_ref[found_ref[block * UNROLL + u]],
                    preferred_element_type=jnp.float32,
                )
            )
        for place, term in zip(places, terms):
            acc_ref[place] += term
        return carry

    lax.fori_loop(0, (count_ref[0] + UNROLL - 1) // UNROLL, step, 0)


def first_kernel(item_ref, found_ref, count_ref, row_ref, a_ref, b_ref, acc_ref):
    acc_ref[...] = jnp.zeros_like(acc_ref)
    add_pairs(item_ref, found_ref, count_ref, row_ref, a_ref, b_ref, acc_ref)


def second_kernel(
    item_ref, found_ref, count_ref, row_ref, place_ref, a_ref, b_ref, start_ref, out_ref, acc_ref
):
    acc_ref[...] = start_ref[...]
    add_pairs(item_ref, found_ref, count_ref, row_ref, a_ref, b_ref, acc_ref)
    rest = acc_ref.shape[-1] - LANES
    out_ref[:, :, BCL * LANES :] = jnp.zeros_like(out_ref[:, :, BCL * LANES :])

    def put(i, carry):
        place = place_ref[i]
        for j in range(BCL):
            block = acc_ref[i * BCL + j].astype(jnp.bfloat16)
            out_ref[place, :, j * LANES : (j + 1) * LANES] = block[:, :LANES]
            out_ref[place, :, BCL * LANES + j * rest : BCL * LANES + (j + 1) * rest] = block[:, LANES:]
        return carry

    lax.fori_loop(0, out_ref.shape[0], put, 0)


def cost(a):
    slots, rows, depth = a.shape
    return pl.CostEstimate(
        flops=2 * slots * rows * 256 * 512, bytes_accessed=8_000_000, transcendentals=0
    )


def first_stop(a, pairs, rows, b):
    return pl.pallas_call(
        first_kernel,
        out_shape=jax.ShapeDtypeStruct((BRL * BCL + 1, a.shape[1], b.shape[-1]), jnp.float32),
        in_specs=[SMEM] * 4 + [VMEM] * 2,
        out_specs=VMEM,
        cost_estimate=cost(a),
        name="first_stop",
    )(*pairs, rows, a, b)


def second_stop(a, pairs, rows, place, b, start):
    return pl.pallas_call(
        second_kernel,
        out_shape=jax.ShapeDtypeStruct((BRL, a.shape[1], (BCL + 1) * LANES), jnp.bfloat16),
        in_specs=[SMEM] * 5 + [VMEM] * 3,
        out_specs=VMEM,
        scratch_shapes=[pltpu.VMEM(start.shape, jnp.float32)],
        cost_estimate=cost(a),
        name="second_stop",
    )(*pairs, rows, place, a, b, start)


def unpack_kernel(src_ref, in_ref, out_ref):
    rest = out_ref.shape[-1] - LANES

    def step(l, carry):
        strip = in_ref[src_ref[l]]
        for j in range(BCL):
            out_ref[l, j, :, 0:LANES] = strip[:, j * LANES : (j + 1) * LANES]
            out_ref[l, j, :, LANES:] = strip[:, BCL * LANES + j * rest : BCL * LANES + (j + 1) * rest]
        return carry

    lax.fori_loop(0, out_ref.shape[0], step, 0)


def unpack(arrived, source, edge):
    return pl.pallas_call(
        unpack_kernel,
        out_shape=jax.ShapeDtypeStruct((BRL, BCL, arrived.shape[1], edge), jnp.bfloat16),
        in_specs=[SMEM, VMEM],
        out_specs=VMEM,
        name="unpack",
    )(source, arrived)


def matches(a_codes, b_codes, keep):
    slots = jnp.arange(b_codes.shape[0], dtype=jnp.int32)
    places = jnp.arange(BCL, dtype=jnp.int32)
    wanted = (a_codes % KL)[:, None] * BCL + places[None, :]
    found = jnp.max(
        jnp.where(wanted[:, :, None] == b_codes[None, None, :], slots[None, None, :], -1), axis=2
    )
    product = (a_codes // KL)[:, None] * BCL + places[None, :]
    kept = jnp.any(product[:, :, None] == keep[None, None, :], axis=2)
    return jnp.where(kept, found, -1).reshape(-1)


def body(a_blocks, a_coord, b_blocks, b_coord, keep_list, permutation):
    row_count = lax.axis_size("row")
    col_count = lax.axis_size("col")
    slot_count = BRL // row_count
    row_here = lax.axis_index("row")
    col_here = lax.axis_index("col")
    row_next = (row_here + 1) % row_count
    col_next = (col_here + 1) % col_count
    edge = a_blocks.shape[-1]
    parts = 3 if edge % 3 == 0 else 1
    size = edge // parts

    as_stored = Layout(major_to_minor=(0, 1, 2))
    a_turned = with_layout_constraint(a_blocks[0, 0].transpose(1, 2, 0), as_stored)
    a_parts = lax.optimization_barrier(
        [
            with_layout_constraint(a_turned[q * size : (q + 1) * size], as_stored)
            for q in range(parts)
        ]
    )
    a_moved = [shifted(part, "col", -1) for part in a_parts]

    b_first = b_blocks[0, 0, 0]
    sent_pick = (row_here == 0).astype(jnp.int32)
    b_sent = lax.optimization_barrier(
        lax.dynamic_index_in_dim(b_blocks[0, :, 0], sent_pick, 0, keepdims=False)
    )
    sent_rest = b_sent[:, :, LANES:].transpose(1, 0, 2).reshape(edge, -1)
    moved_main = shifted(b_sent[:, :, :LANES], "row", -1)
    moved_rest = shifted(sent_rest, "row", -1)
    moved_rest = moved_rest.reshape(edge, b_first.shape[0], -1).transpose(1, 0, 2)

    own_keep = keep_list[row_here, col_here]
    a_codes1, a_codes2 = a_coord[row_here, col_here], a_coord[row_here, col_next]
    image_pick = (row_next == 0).astype(jnp.int32)
    pairs1 = list_pairs(matches(a_codes1, b_coord[row_here, 0, col_here], own_keep))
    pairs2 = list_pairs(matches(a_codes2, b_coord[row_next, image_pick, col_here], own_keep))
    rows1, rows2 = a_codes1 // KL, a_codes2 // KL

    targets = permutation.reshape(row_count, BRL)
    owners = targets // BRL
    positions = jnp.arange(BRL, dtype=jnp.int32)
    before = (owners[:, None, :] == owners[:, :, None]) & (
        positions[None, None, :] < positions[None, :, None]
    )
    slot_rank = jnp.sum(before.astype(jnp.int32), axis=2)
    place = owners[row_here] * slot_count + slot_rank[row_here]
    all_rows = jnp.arange(permutation.shape[0], dtype=jnp.int32)
    wanted = row_here * BRL + positions
    arrival = all_rows // BRL * slot_count + slot_rank.reshape(-1)
    source = jnp.sum(
        jnp.where(permutation[None, :] == wanted[:, None], arrival[None, :], 0), axis=1
    )

    starts = [first_stop(part.transpose(2, 0, 1), pairs1, rows1, b_first) for part in a_parts]
    b_moved = jnp.concatenate([moved_main, moved_rest], axis=2)
    done = []
    for q in range(parts):
        out = second_stop(
            a_moved[q].transpose(2, 0, 1), pairs2, rows2, place, b_moved, starts[q]
        )
        incoming = lax.all_to_all(out, "row", split_axis=0, concat_axis=0, tiled=True)
        done.append(unpack(incoming, source, edge))
    return jnp.concatenate(done, axis=2)[None, None]


def solution(mesh):
    in_specs = (
        P("row", "col", None, None, None),
        P(),
        P("row", None, "col", None, None, None),
        P(),
        P(),
        P(),
    )
    out_specs = P("row", "col", None, None, None, None)
    return jax.shard_map(body, mesh=mesh, in_specs=in_specs, out_specs=out_specs, check_vma=False)
```

```python
import jax
import jax.numpy as jnp
from jax import lax
from jax.experimental.layout import Layout, with_layout_constraint
from jax.experimental import pallas as pl
from jax.experimental.pallas import tpu as pltpu
from jax.sharding import PartitionSpec as P

KL = 72
BRL = 16
BCL = 4
LANES = 128
UNROLL = 8
SMEM = pl.BlockSpec(memory_space=pltpu.SMEM)
VMEM = pl.BlockSpec(memory_space=pltpu.VMEM)


def shifted(value, axis, steps):
    count = lax.axis_size(axis)
    pairs = [(source, (source + steps) % count) for source in range(count)]
    return lax.ppermute(value, axis, pairs)


def list_kernel(match_ref, item_ref, found_ref, count_ref):
    def step(n, at):
        slot = match_ref[n]
        item_ref[at] = n
        found_ref[at] = slot
        return at + (slot >= 0).astype(jnp.int32)

    total = lax.fori_loop(0, match_ref.shape[0], step, jnp.int32(0), unroll=8)
    count_ref[0] = total
    for extra in range(UNROLL):
        item_ref[total + extra] = -1
        found_ref[total + extra] = 0


def list_pairs(match):
    length = match.shape[0] + UNROLL
    shape = jax.ShapeDtypeStruct((length,), jnp.int32)
    return pl.pallas_call(
        list_kernel,
        out_shape=(shape, shape, jax.ShapeDtypeStruct((1,), jnp.int32)),
        in_specs=[SMEM],
        out_specs=(SMEM, SMEM, SMEM),
        name="list_pairs",
    )(match)


def add_pairs(item_ref, found_ref, count_ref, row_ref, a_ref, b_ref, acc_ref):
    spare = acc_ref.shape[0] - 1

    def step(block, carry):
        terms, places = [], []
        for u in range(UNROLL):
            item = item_ref[block * UNROLL + u]
            real = item >= 0
            safe = jnp.maximum(item, 0)
            s = safe // BCL
            places.append(jnp.where(real, row_ref[s] * BCL + safe % BCL, spare))
            terms.append(
                jnp.dot(
                    a_ref[s],
                    b_ref[found_ref[block * UNROLL + u]],
                    preferred_element_type=jnp.float32,
                )
            )
        for place, term in zip(places, terms):
            acc_ref[place] += term
        return carry

    lax.fori_loop(0, (count_ref[0] + UNROLL - 1) // UNROLL, step, 0)


def first_kernel(item_ref, found_ref, count_ref, row_ref, a_ref, b_ref, acc_ref):
    acc_ref[...] = jnp.zeros_like(acc_ref)
    add_pairs(item_ref, found_ref, count_ref, row_ref, a_ref, b_ref, acc_ref)


def second_kernel(
    item_ref, found_ref, count_ref, row_ref, place_ref, a_ref, b_ref, start_ref, out_ref, acc_ref
):
    acc_ref[...] = start_ref[...]
    add_pairs(item_ref, found_ref, count_ref, row_ref, a_ref, b_ref, acc_ref)
    rest = acc_ref.shape[-1] - LANES
    out_ref[:, :, BCL * LANES :] = jnp.zeros_like(out_ref[:, :, BCL * LANES :])

    def put(i, carry):
        place = place_ref[i]
        for j in range(BCL):
            block = acc_ref[i * BCL + j].astype(jnp.bfloat16)
            out_ref[place, :, j * LANES : (j + 1) * LANES] = block[:, :LANES]
            out_ref[place, :, BCL * LANES + j * rest : BCL * LANES + (j + 1) * rest] = block[:, LANES:]
        return carry

    lax.fori_loop(0, out_ref.shape[0], put, 0)


def cost(a):
    slots, rows, depth = a.shape
    return pl.CostEstimate(
        flops=2 * slots * rows * 256 * 512, bytes_accessed=8_000_000, transcendentals=0
    )


def first_stop(a, pairs, rows, b):
    return pl.pallas_call(
        first_kernel,
        out_shape=jax.ShapeDtypeStruct((BRL * BCL + 1, a.shape[1], b.shape[-1]), jnp.float32),
        in_specs=[SMEM] * 4 + [VMEM] * 2,
        out_specs=VMEM,
        cost_estimate=cost(a),
        name="first_stop",
    )(*pairs, rows, a, b)


def second_stop(a, pairs, rows, place, b, start):
    return pl.pallas_call(
        second_kernel,
        out_shape=jax.ShapeDtypeStruct((BRL, a.shape[1], (BCL + 1) * LANES), jnp.bfloat16),
        in_specs=[SMEM] * 5 + [VMEM] * 3,
        out_specs=VMEM,
        scratch_shapes=[pltpu.VMEM(start.shape, jnp.float32)],
        cost_estimate=cost(a),
        name="second_stop",
    )(*pairs, rows, place, a, b, start)


def unpack_kernel(src_ref, in_ref, out_ref):
    rest = out_ref.shape[-1] - LANES

    def step(l, carry):
        strip = in_ref[src_ref[l]]
        for j in range(BCL):
            out_ref[l, j, :, 0:LANES] = strip[:, j * LANES : (j + 1) * LANES]
            out_ref[l, j, :, LANES:] = strip[:, BCL * LANES + j * rest : BCL * LANES + (j + 1) * rest]
        return carry

    lax.fori_loop(0, out_ref.shape[0], step, 0)


def unpack(arrived, source, edge):
    return pl.pallas_call(
        unpack_kernel,
        out_shape=jax.ShapeDtypeStruct((BRL, BCL, arrived.shape[1], edge), jnp.bfloat16),
        in_specs=[SMEM, VMEM],
        out_specs=VMEM,
        name="unpack",
    )(source, arrived)


def matches(a_codes, b_codes, keep):
    slots = jnp.arange(b_codes.shape[0], dtype=jnp.int32)
    places = jnp.arange(BCL, dtype=jnp.int32)
    wanted = (a_codes % KL)[:, None] * BCL + places[None, :]
    found = jnp.max(
        jnp.where(wanted[:, :, None] == b_codes[None, None, :], slots[None, None, :], -1), axis=2
    )
    product = (a_codes // KL)[:, None] * BCL + places[None, :]
    kept = jnp.any(product[:, :, None] == keep[None, None, :], axis=2)
    return jnp.where(kept, found, -1).reshape(-1)


def body(a_blocks, a_coord, b_blocks, b_coord, keep_list, permutation):
    row_count = lax.axis_size("row")
    col_count = lax.axis_size("col")
    slot_count = BRL // row_count
    row_here = lax.axis_index("row")
    col_here = lax.axis_index("col")
    row_next = (row_here + 1) % row_count
    col_next = (col_here + 1) % col_count
    edge = a_blocks.shape[-1]
    parts = 3 if edge % 3 == 0 else 1
    size = edge // parts

    as_stored = Layout(major_to_minor=(0, 1, 2))
    a_turned = with_layout_constraint(a_blocks[0, 0].transpose(1, 2, 0), as_stored)
    a_parts = lax.optimization_barrier(
        [
            with_layout_constraint(a_turned[q * size : (q + 1) * size], as_stored)
            for q in range(parts)
        ]
    )
    a_moved = [shifted(part, "col", -1) for part in a_parts]

    b_first = b_blocks[0, 0, 0]
    sent_pick = (row_here == 0).astype(jnp.int32)
    b_sent = lax.optimization_barrier(
        lax.dynamic_index_in_dim(b_blocks[0, :, 0], sent_pick, 0, keepdims=False)
    )
    sent_rest = b_sent[:, :, LANES:].transpose(1, 0, 2).reshape(edge, -1)
    moved_main = shifted(b_sent[:, :, :LANES], "row", -1)
    moved_rest = shifted(sent_rest, "row", -1)
    moved_rest = moved_rest.reshape(edge, b_first.shape[0], -1).transpose(1, 0, 2)

    own_keep = keep_list[row_here, col_here]
    a_codes1, a_codes2 = a_coord[row_here, col_here], a_coord[row_here, col_next]
    image_pick = (row_next == 0).astype(jnp.int32)
    pairs1 = list_pairs(matches(a_codes1, b_coord[row_here, 0, col_here], own_keep))
    pairs2 = list_pairs(matches(a_codes2, b_coord[row_next, image_pick, col_here], own_keep))
    rows1, rows2 = a_codes1 // KL, a_codes2 // KL

    targets = permutation.reshape(row_count, BRL)
    owners = targets // BRL
    positions = jnp.arange(BRL, dtype=jnp.int32)
    before = (owners[:, None, :] == owners[:, :, None]) & (
        positions[None, None, :] < positions[None, :, None]
    )
    slot_rank = jnp.sum(before.astype(jnp.int32), axis=2)
    place = owners[row_here] * slot_count + slot_rank[row_here]
    all_rows = jnp.arange(permutation.shape[0], dtype=jnp.int32)
    wanted = row_here * BRL + positions
    arrival = all_rows // BRL * slot_count + slot_rank.reshape(-1)
    source = jnp.sum(
        jnp.where(permutation[None, :] == wanted[:, None], arrival[None, :], 0), axis=1
    )

    starts = [first_stop(part.transpose(2, 0, 1), pairs1, rows1, b_first) for part in a_parts]
    b_moved = jnp.concatenate([moved_main, moved_rest], axis=2)
    done = []
    for q in range(parts):
        out = second_stop(
            a_moved[q].transpose(2, 0, 1), pairs2, rows2, place, b_moved, starts[q]
        )
        incoming = lax.all_to_all(out, "row", split_axis=0, concat_axis=0, tiled=True)
        done.append(unpack(incoming, source, edge))
    return jnp.concatenate(done, axis=2)[None, None]


def solution(mesh):
    in_specs = (
        P("row", "col", None, None, None),
        P(),
        P("row", None, "col", None, None, None),
        P(),
        P(),
        P(),
    )
    out_specs = P("row", "col", None, None, None, None)
    return jax.shard_map(body, mesh=mesh, in_specs=in_specs, out_specs=out_specs, check_vma=False)
```
